32 devices in a mesh: scen: 4 (over y, x), opt: 8 (over z, core).
Axes of the slice: x: 2, y: 2, z: 4, core: 2. Of those that a mesh axis runs over, the one named last changes fastest.
Arguments:
- option_coefs: float32 [4096, 1024], P(('opt', 'scen')), may hold values from -0.75 to 0.75
- underlying_of: int32 [4096, 1], P('opt'), may hold values from 0 to 31; in each aligned block of 128 rows (0 to 127, 128 to 255, ...) at most 8 rows name the same one
- log_return_mean: float32 [32, 1024], P(('scen', 'opt')), may hold values from -1 to 1
- log_return_spread: float32 [32, 1024], P(('scen', 'opt')), may hold values from 1e-06 to 0.0001
- cost: float32 [4096], P('opt'), may hold values from -3 to 3
- positions: float32 [4096], P('opt'), may hold values from -1 to 1
- base_loss: float32 [1024], P('scen'), may hold values from -6 to 6
- duals: float32 [1024], P('scen'), may hold values from 0 to 1
- threshold: float32 [1], replicated, may hold values from -2 to 2
Outputs:
- scenario_values: float32 [4096, 1024], P('opt', 'scen')
- new_positions: float32 [4096], P('opt')
- new_duals: float32 [1024], P('scen')
- new_threshold: float32 [1], replicated
The draws below stay inside these ranges and needn't reach their ends.
Inputs may be any that keep to these rules, and one draw needn't show every extreme that they name: `underlying_of`: in each aligned block of 128 options no underlying is named more than 8 times, a bound that some block reaches; every underlying is named somewhere.
All inputs are finite; a program needn't handle non-finite values.
Results may differ from the reference program's by a relative error of at most 0.0003.
Values sent between devices are 32-bit elements; how exact they have to be, the bound alone decides.
A program may use at most 64 MiB of HBM per device.

```python
import math
import jax
import jax.numpy as jnp
import numpy as np
from jax import lax

TERMS = 1024
OPT_DEV = 128
ITERS = 2
SCENARIOS = 1024
OPTIONS = 4096
UNDERLYINGS = 32
MOST = 8


def draw_duals(key, part):
    position = jnp.arange(SCENARIOS, dtype=jnp.float32) / SCENARIOS
    rising = 0.25 + 0.75 * position
    uniform_draw = jax.random.uniform(key, (SCENARIOS,), jnp.float32, 0.0, 1.0)
    return jnp.clip(rising * uniform_draw, 0.0, 1.0)


def level_of(rng, dims, cuts, smallest, high):
    level = 1.0
    for axis_at, parts in cuts:
        draws = jax.random.uniform(jax.random.fold_in(jax.random.fold_in(rng, 6), axis_at), (parts,), jnp.float32, smallest / len(cuts), high / len(cuts))
        level = level * jnp.repeat(jnp.exp(draws), dims[axis_at] // parts).reshape((-1,) + (1,) * (len(dims) - 1 - axis_at))
    return level


def shared_out(key, own, number, rows, amount, top, limit, slope):
    ranking = jax.random.permutation(key, amount)
    heavy_load, usual = shares(amount, rows * top, limit, slope, True), shares(amount, rows * top, limit, slope, False)
    places = jnp.arange(amount)

    def named(sizes, offset_by):
        used = int((sizes > 0).sum())
        fixed = max(1, used // 4)
        shifted = fixed + (places - fixed + offset_by * (used - fixed)) % max(1, amount - fixed)
        return jnp.zeros((amount,), jnp.int32).at[ranking[jnp.where(places < fixed, places, shifted)]].set(jnp.asarray(sizes, jnp.int32))

    sizes = jnp.where(number % 4 == 0, named(heavy_load, number // 4), named(usual, number - number // 4 - 1))
    mixed = jax.random.permutation(jax.random.fold_in(own, 3), amount)
    source_of, taker = mixed[0:amount // 2 * 2:2], mixed[1:amount // 2 * 2:2]
    slack = jnp.minimum(sizes[source_of] - 1, limit - sizes[taker]) // 2
    slack = jnp.where((source_of == ranking[0]) | (taker == ranking[0]) | (sizes[taker] == 0), 0, jnp.maximum(slack, 0))
    shifted = jax.random.randint(jax.random.fold_in(own, 4), (amount // 2,), 0, 1 << 20) % (slack + 1)
    sizes = sizes.at[source_of].add(-shifted).at[taker].add(shifted)
    items = jnp.searchsorted(jnp.cumsum(sizes), jnp.arange(rows * top), side="right").astype(jnp.int32)
    table = items.reshape(top, rows).T
    table = table[jax.random.permutation(jax.random.fold_in(own, 1), rows)]
    offset_by = jax.random.randint(jax.random.fold_in(own, 2), (rows, 1), 0, top)
    return jnp.take_along_axis(table, (jnp.arange(top)[None, :] + offset_by) % top, axis=1)


def shares(amount, total, limit, skew, full):
    weights = [(1 << 20) // math.isqrt(rank ** skew) + 1 for rank in range(1, amount + 1)]
    largest = limit if full else min(limit, max(-(-total // amount), total * weights[0] // sum(weights)))
    least = 1 if total - largest >= amount - 1 else 0
    given, surplus = [largest] + [least] * (amount - 1), total - largest - least * (amount - 1)
    while surplus > 0:
        movable = [i for i in range(1, amount) if given[i] < largest] or [i for i in range(1, amount) if given[i] < limit]
        mass, budget = sum([weights[i] for i in movable]), surplus
        for i in movable:
            addition = min(limit - given[i], max(1, budget * weights[i] // mass), surplus)
            given[i] = given[i] + addition
            surplus = surplus - addition
    return np.array(given)


def centred(key, extent, scale, bound, split=(), kind=jnp.bfloat16):
    gain = level_of(key, extent, split, -0.22, 0.18) if split else 1.0
    drawn = jax.random.normal(key, extent, jnp.float32) * scale * gain
    return jnp.minimum(jnp.maximum(drawn, -bound), bound).astype(kind)


def setup_inputs(seed: int = 0) -> dict:
    keys = jax.random.split(jax.random.key(seed), 10)
    option_coefs = centred(keys[0], (OPTIONS, TERMS), 0.125, 0.75, ((0, 32),), jnp.float32)
    underlying_of_keys = jax.random.split(jax.random.fold_in(keys[1], 1), OPTIONS // OPT_DEV)
    underlying_of_turns = jax.random.permutation(jax.random.fold_in(keys[1], 3), OPTIONS // OPT_DEV)
    underlying_of = jax.vmap(lambda own, number: shared_out(jax.random.fold_in(keys[1], 2), own, number, OPT_DEV, UNDERLYINGS, 1, MOST, 2))(underlying_of_keys, underlying_of_turns).reshape((OPTIONS, 1))
    log_return_mean = jnp.clip(jax.random.uniform(keys[2], (UNDERLYINGS, SCENARIOS), jnp.float32, -1.0, 1.0) * level_of(keys[2], (UNDERLYINGS, SCENARIOS), ((0, 32),), -0.4, 0.0), -1.0, 1.0)
    log_return_spread = jnp.clip(jnp.exp(math.log(0.0001) - 4.6051702 * jax.random.uniform(keys[3], (UNDERLYINGS, SCENARIOS), jnp.float32) ** level_of(keys[3], (UNDERLYINGS, SCENARIOS), ((0, 32),), -0.2, 0.2)), 9.999999974752427e-07, 0.0001)
    cost = centred(keys[4], (OPTIONS,), 0.5, 3.0, ((0, 8),), jnp.float32)
    positions = jnp.clip(jax.random.uniform(keys[5], (OPTIONS,), jnp.float32, -1.0, 1.0) * level_of(keys[5], (OPTIONS,), ((0, 8),), -0.4, 0.0), -1.0, 1.0)
    base_loss = centred(keys[6], (SCENARIOS,), 1.0, 6.0, ((0, 4),), jnp.float32)
    duals = draw_duals(jax.random.fold_in(keys[9], 71), 0)
    threshold = centred(keys[8], (1,), 0.5, 2.0, (), jnp.float32)
    return dict(option_coefs=option_coefs, underlying_of=underlying_of, log_return_mean=log_return_mean, log_return_spread=log_return_spread, cost=cost, positions=positions, base_loss=base_loss, duals=duals, threshold=threshold)


LOW_END = -4.0
HIGH_END = 4.0
TAIL_LEVEL = 0.9
PRIMAL_STEP = 0.5
THRESH_STEP = 0.05
DUAL_STEP = 0.5

def cosine_terms(drift_rows, variance_rows, term_count):
    frequency = jnp.arange(term_count, dtype=jnp.float32) * (math.pi / (HIGH_END - LOW_END))
    weight = jnp.where(jnp.arange(term_count) == 0, 0.5, 1.0).astype(jnp.float32) * (2.0 / (HIGH_END - LOW_END))
    decay = jnp.exp(-0.5 * variance_rows[:, None] * frequency * frequency)
    return weight * decay * jnp.cos(frequency * (drift_rows[:, None] - LOW_END))

def reference(option_coefs, underlying_of, log_return_mean, log_return_spread, cost, positions, base_loss, duals, threshold):
    owners = underlying_of[:, 0].reshape(-1, OPT_DEV)
    blocks = owners.shape[0]
    onehot = (owners[..., None] == jnp.arange(UNDERLYINGS, dtype=jnp.int32)).astype(jnp.int32)
    slot_rank = lax.optimization_barrier(jnp.sum((jnp.cumsum(onehot, axis=1) - onehot) * onehot, axis=-1))
    place_offset_number = (jnp.arange(blocks, dtype=jnp.int32)[:, None] * MOST + slot_rank).reshape(-1).astype(jnp.int32)
    linear_holder_number = owners.reshape(-1).astype(jnp.int32)
    resorted_worths = jnp.zeros((UNDERLYINGS, blocks * MOST, TERMS), jnp.float32).at[linear_holder_number, place_offset_number].set(option_coefs)

    def contract_cost_holder(operands):
        drift_rows, variance_rows, coef_rows = operands
        cosine_table = cosine_terms(drift_rows, variance_rows, TERMS)
        return jnp.dot(coef_rows, cosine_table.T, precision=lax.Precision.HIGHEST)
    valued_contracts = lax.map(contract_cost_holder, (log_return_mean, log_return_spread, resorted_worths))
    contract_worths = valued_contracts[linear_holder_number, place_offset_number]
    holding = positions
    weights = duals
    level = threshold[0]
    for iteration in range(ITERS):
        gradient = cost - jnp.dot(contract_worths, weights, precision=lax.Precision.HIGHEST) / math.sqrt(SCENARIOS)
        dual_mass = jnp.sum(weights)
        holding_next = jnp.clip(holding - PRIMAL_STEP * gradient, -1.0, 1.0)
        level_next = level - THRESH_STEP * (1.0 - dual_mass / ((1.0 - TAIL_LEVEL) * SCENARIOS))
        holding_bar = 2.0 * holding_next - holding
        level_bar = 2.0 * level_next - level
        pnl = jnp.dot(holding_bar, contract_worths, precision=lax.Precision.HIGHEST) / math.sqrt(OPTIONS)
        weights = jnp.clip(weights + DUAL_STEP * (base_loss - pnl - level_bar), 0.0, 1.0)
        holding = holding_next
        level = level_next
    return (contract_worths, holding, weights, level.reshape(1))
```

```python
import functools
import math

import jax
import jax.numpy as jnp
from jax import lax
from jax.experimental import pallas as pl
from jax.experimental.pallas import tpu as pltpu
from jax.sharding import PartitionSpec as P

ITERS = 2

LOW_END = -4.0
HIGH_END = 4.0
TAIL_LEVEL = 0.9
PRIMAL_STEP = 0.5
THRESH_STEP = 0.05
DUAL_STEP = 0.5

MESH = pl.DeviceIdType.MESH
CHUNK = 256
STEM = 64
F32 = jnp.float32
BF16 = jnp.bfloat16


def flip(index, bits):
    out = index
    place = 1
    while place <= bits:
        if bits & place:
            bit = lax.rem(index // place, 2)
            out = out + place * (1 - 2 * bit)
        place *= 2
    return out


def halves(x):
    high = x.astype(BF16)
    low = (x - high.astype(F32)).astype(BF16)
    return high, low


def turn(x):
    x = x - jnp.floor(x + 0.5)
    h = x * math.pi
    z = h * h
    s = F32(-1.0 / 39916800.0)
    for c in (1.0 / 362880.0, -1.0 / 5040.0, 1.0 / 120.0, -1.0 / 6.0, 1.0):
        s = s * z + F32(c)
    s = s * h
    c_ = F32(1.0 / 479001600.0)
    for c in (-1.0 / 3628800.0, 1.0 / 40320.0, -1.0 / 720.0, 1.0 / 24.0, -0.5, 1.0):
        c_ = c_ * z + F32(c)
    return 1.0 - 2.0 * s * s, 2.0 * s * c_


def kernel(
    dims,
    coef, prm_in, urow, ucol, cost, pos, base, dual, thr,
    val_out, x_out, y_out, z_out,
    F, prm, base_c, base_s, stem_c, stem_s, ksq, Pm, PT, fhl, Fs, acc, ahl, VH, VL,
    gst, gbuf, pst, pbuf,
    ag_send, ag_recv, own_sem, prm_own, pa_send, pa_recv, pb_send, pb_recv,
    g_send, g_recv, p_send, p_recv,
):
    S, O, limit = dims
    D = S * O
    B, T = coef.shape
    SC = base.shape[1]
    NJ = S * B
    SL = S * limit
    R = D * SL
    KC = F.shape[3]
    NK = T // KC
    Q = KC // STEM
    H = B // 2
    n = S.bit_length() - 1
    me = lax.axis_index("scen")
    col = lax.axis_index("opt")

    barrier = pltpu.get_barrier_semaphore()
    for e in range(1, S):
        pl.semaphore_signal(barrier, inc=1, device_id=(flip(me, e), col), device_id_type=MESH)
    for e in range(1, O):
        pl.semaphore_signal(barrier, inc=1, device_id=(me, flip(col, e)), device_id_type=MESH)
    pl.semaphore_wait(barrier, S + O - 2)

    def prm_a(e):
        peer = flip(me, e)
        return pltpu.make_async_remote_copy(
            src_ref=prm_in.at[peer], dst_ref=prm.at[col, me],
            send_sem=pa_send.at[e], recv_sem=pa_recv.at[e],
            device_id=(peer, col), device_id_type=MESH)

    def prm_b(e):
        peer = flip(col, e)
        return pltpu.make_async_remote_copy(
            src_ref=prm.at[col], dst_ref=prm.at[col],
            send_sem=pb_send.at[e], recv_sem=pb_recv.at[e],
            device_id=(me, peer), device_id_type=MESH)

    for e in range(1, S):
        prm_a(e).start()
    prm_mine = pltpu.make_async_copy(prm_in.at[me], prm.at[col, me], prm_own)
    prm_mine.start()

    def piece(kc, h, held, d):
        block = flip(me, held)
        rows = pl.ds(h * H, H)
        if held == 0:
            src = coef.at[rows, pl.ds(kc * KC, KC)]
        else:
            src = F.at[kc, block, rows]
        to = held ^ (1 << d)
        return pltpu.make_async_remote_copy(
            src_ref=src, dst_ref=F.at[kc, block, rows],
            send_sem=ag_send.at[kc, h, to], recv_sem=ag_recv.at[kc, h, to],
            device_id=(flip(me, 1 << d), col), device_id_type=MESH)

    def landed(kc, h, e):
        slot = F.at[kc, flip(me, e), pl.ds(h * H, H)]
        pltpu.make_async_remote_copy(
            src_ref=slot, dst_ref=slot,
            send_sem=ag_send.at[kc, h, e], recv_sem=ag_recv.at[kc, h, e],
            device_id=(flip(me, 1), col), device_id_type=MESH).wait_recv()

    orders = [[(h + i) % n for i in range(n)] for h in range(2)]

    def plan(h):
        out = [(0, orders[h])]
        for i, d in enumerate(orders[h]):
            out += [(held ^ (1 << d), orders[h][i + 1:]) for held, _ in list(out)]
        return out

    def own(kc):
        for i in range(n):
            for h in range(2):
                piece(kc, h, 0, orders[h][i]).start()
        pltpu.make_async_copy(
            coef.at[:, pl.ds(kc * KC, KC)], F.at[kc, me], own_sem.at[kc]).start()

    def forward(kc):
        plans = [plan(h) for h in range(2)]
        for i in range(1, S):
            for h in range(2):
                held, later = plans[h][i]
                if later:
                    landed(kc, h, held)
                    for d in later:
                        piece(kc, h, held, d).start()

    def complete(kc):
        for h in range(2):
            for held, later in plan(h)[1:]:
                if not later:
                    landed(kc, h, held)
        pltpu.make_async_copy(
            coef.at[:, pl.ds(kc * KC, KC)], F.at[kc, me], own_sem.at[kc]).wait()

    own(0)
    if NK > 1:
        own(1)

    prm_mine.wait()
    for e in range(1, S):
        prm_a(e).wait_recv()
    for e in range(1, O):
        prm_b(e).start()

    sub = lax.broadcasted_iota(jnp.int32, (B, B), 0)
    lane = lax.broadcasted_iota(jnp.int32, (B, B), 1)
    for b in range(S):
        ur = urow[b].astype(F32)
        uc = ucol[b * B:(b + 1) * B, :].astype(F32)
        same = uc == ur
        rank_r = jnp.sum(jnp.where(same & (sub < lane), 1.0, 0.0), axis=0, keepdims=True)
        rank_c = jnp.sum(jnp.where(same & (lane < sub), 1.0, 0.0), axis=1, keepdims=True)
        place_r = (ur * SL + (rank_r + float(b * limit))).astype(jnp.int32)
        place_c = (uc * SL + (rank_c + float(b * limit))).astype(jnp.int32)
        Pm[:, b * B:(b + 1) * B] = jnp.where(
            lax.broadcasted_iota(jnp.int32, (R, B), 0) == place_r, 1.0, 0.0).astype(BF16)
        PT[b * B:(b + 1) * B, :] = jnp.where(
            lax.broadcasted_iota(jnp.int32, (B, R), 1) == place_c, 1.0, 0.0).astype(BF16)
    term = lax.broadcasted_iota(jnp.int32, (T, SC), 0).astype(F32)
    ksq[...] = term * term

    forward(0)
    if NK > 2:
        own(2)
    for e in range(1, O):
        prm_b(e).wait_recv()

    NB = T // STEM
    idx = lax.broadcasted_iota(jnp.int32, (16 + NB, SC), 0)
    kv = jnp.where(idx < 8, idx, jnp.where(idx == 8, 8, jnp.where(idx == 9, 16, jnp.where(idx == 10, 32, 0))))
    kv = jnp.where(idx >= 16, STEM * (idx - 16), kv).astype(F32)

    def stems(u, carry):
        mean = prm[lax.rem(u, O), u // O][0:1, :]
        x = (mean - LOW_END) * (0.5 / (HIGH_END - LOW_END))
        xh = jnp.floor(x * 4096.0 + 0.5) * (1.0 / 4096.0)
        xl = x - xh
        ph = kv * xh
        ph = ph - jnp.floor(ph + 0.5)
        c, s = turn(ph + kv * xl)
        base_c[u] = c[16:]
        base_s[u] = s[16:]
        cs, ss = c[0:8], s[0:8]
        for i in range(3):
            c1, s1 = c[8 + i:9 + i], s[8 + i:9 + i]
            cs, ss = (jnp.concatenate([cs, cs * c1 - ss * s1], 0),
                      jnp.concatenate([ss, ss * c1 + cs * s1], 0))
        stem_c[u] = cs
        stem_s[u] = ss
        return carry

    lax.fori_loop(0, D, stems, 0)
    if NK > 1:
        forward(1)
    if NK > 3:
        own(3)
    for kc in range(4, NK):
        own(kc)

    RB = 128
    freq2 = -0.5 * (math.pi / (HIGH_END - LOW_END)) ** 2 / math.log(2.0)
    for kc in range(NK):
        complete(kc)
        if kc + 2 < NK:
            forward(kc + 2)
        for b in range(S):
            f = F[kc, b] * (2.0 / (HIGH_END - LOW_END))
            if kc == 0:
                f = jnp.where(lax.broadcasted_iota(jnp.int32, (B, KC), 1) == 0, f * 0.5, f)
            hi, lo = halves(f)
            fhl[b * B:(b + 1) * B, 0:KC] = hi
            fhl[b * B:(b + 1) * B, KC:2 * KC] = lo

        def arrange(r, carry):
            got = jnp.dot(Pm[pl.ds(pl.multiple_of(r * RB, RB), RB), :], fhl[...],
                          preferred_element_type=F32).astype(BF16)
            per = RB // SL
            at = pl.ds(r * per, per)
            Fs[at, 0:SL, :] = got[:, 0:KC].reshape(per, SL, KC)
            Fs[at, SL:2 * SL, :] = got[:, KC:].reshape(per, SL, KC)
            return carry

        lax.fori_loop(0, R // RB, arrange, 0)

        def price(u, carry):
            decay = prm[lax.rem(u, O), u // O][1:2, :] * freq2
            highs, lows = [], []
            for q in range(Q):
                g = kc * Q + q
                c = base_c[u, g:g + 1, :] * stem_c[u] - base_s[u, g:g + 1, :] * stem_s[u]
                v = c * jnp.exp2(decay * ksq[g * STEM:(g + 1) * STEM, :])
                hi, lo = halves(v)
                highs.append(hi)
                lows.append(lo)
            both = jnp.dot(Fs[u], jnp.concatenate(highs, 0), preferred_element_type=F32)
            low = jnp.dot(Fs[u, 0:SL, :], jnp.concatenate(lows, 0), preferred_element_type=F32)
            total = both[0:SL] + (both[SL:] + low)
            acc[u] = total if kc == 0 else acc[u] + total
            return carry

        lax.fori_loop(0, D, price, 0, unroll=2)

    def spread_halves(u, carry):
        hi, lo = halves(acc[u])
        at = pl.ds(pl.multiple_of(u * SL, SL), SL)
        ahl[at, 0:SC] = hi
        ahl[at, SC:2 * SC] = lo
        return carry

    lax.fori_loop(0, D, spread_halves, 0)

    def restore(r, carry):
        at = pl.ds(pl.multiple_of(r * B, B), B)
        got = jnp.dot(PT[at, :], ahl[...], preferred_element_type=F32)
        val_out[at, :] = got[:, 0:SC] + got[:, SC:]
        VH[at, :] = got[:, 0:SC].astype(BF16)
        VL[at, :] = got[:, SC:].astype(BF16)
        return carry

    lax.fori_loop(0, S, restore, 0)

    def pair(row):
        hi = row.astype(BF16).astype(F32)
        at = lax.broadcasted_iota(jnp.int32, (16, row.shape[1]), 0)
        return jnp.where(at == 0, hi, jnp.where(at == 1, row - hi, 0.0)).astype(BF16)

    def product(row, contract):
        lhs = pair(row)
        dn = (((1,), (contract,)), ((), ()))
        out = lax.dot_general(lhs, VH[...], dn, preferred_element_type=F32)
        out = out + lax.dot_general(lhs, VL[...], dn, preferred_element_type=F32)
        return out[0:1] + out[1:2]

    root_scen = math.sqrt(S * SC)
    root_opt = math.sqrt(O * NJ)
    tail = (1.0 - TAIL_LEVEL) * (S * SC)
    x = pos[...]
    y = dual[...]
    z = thr[...]

    def g_copy(it, e):
        return pltpu.make_async_remote_copy(
            src_ref=gst.at[it], dst_ref=gbuf.at[it, me],
            send_sem=g_send.at[it, e], recv_sem=g_recv.at[it, e],
            device_id=(flip(me, e), col), device_id_type=MESH)

    def p_copy(it, e):
        return pltpu.make_async_remote_copy(
            src_ref=pst.at[it], dst_ref=pbuf.at[it, col],
            send_sem=p_send.at[it, e], recv_sem=p_recv.at[it, e],
            device_id=(me, flip(col, e)), device_id_type=MESH)

    for it in range(ITERS):
        part = product(y, 1)
        mass = jnp.broadcast_to(jnp.sum(y, axis=1, keepdims=True), (1, 128))
        gst[it, :, 0:NJ] = part
        gst[it, :, NJ:] = mass
        for e in range(1, S):
            g_copy(it, e).start()
        gbuf[it, me] = gst[it]
        for e in range(1, S):
            g_copy(it, e).wait_recv()
        g = gbuf[it, 0]
        for s in range(1, S):
            g = g + gbuf[it, s]
        x_new = jnp.clip(x - PRIMAL_STEP * (cost[...] - g[:, 0:NJ] / root_scen), -1.0, 1.0)
        z_new = z - THRESH_STEP * (1.0 - g[:, NJ:NJ + 1] / tail)
        x_bar = 2.0 * x_new - x
        z_bar = 2.0 * z_new - z
        pst[it] = product(x_bar, 0)
        for e in range(1, O):
            p_copy(it, e).start()
        pbuf[it, col] = pst[it]
        for e in range(1, O):
            p_copy(it, e).wait_recv()
        p = pbuf[it, 0]
        for o in range(1, O):
            p = p + pbuf[it, o]
        y = jnp.clip(y + DUAL_STEP * (base[...] - p / root_opt - z_bar), 0.0, 1.0)
        x, z = x_new, z_new
    x_out[...] = x
    y_out[...] = y
    z_out[...] = z

    for e in range(1, S):
        prm_a(e).wait_send()
    for e in range(1, O):
        prm_b(e).wait_send()
    for kc in range(NK):
        for h in range(2):
            for held, later in plan(h):
                for d in later:
                    piece(kc, h, held, d).wait_send()
    for it in range(ITERS):
        for e in range(1, S):
            g_copy(it, e).wait_send()
        for e in range(1, O):
            p_copy(it, e).wait_send()


def on_device(
    option_coefs,
    underlying_of,
    log_return_mean,
    log_return_spread,
    cost,
    positions,
    base_loss,
    duals,
    threshold,
):
    S = lax.axis_size("scen")
    O = lax.axis_size("opt")
    D = S * O
    B, T = option_coefs.shape
    SC = duals.shape[0]
    NJ = S * B
    limit = max(2, 2 * B // D)
    SL = S * limit
    R = D * SL
    KC = min(CHUNK, T)
    NK = T // KC
    prm_in = jnp.stack([log_return_mean.reshape(S, SC), log_return_spread.reshape(S, SC)], 1)
    vmem = pl.BlockSpec(memory_space=pltpu.VMEM)
    dma = pltpu.SemaphoreType.DMA
    values, x, y, z = pl.pallas_call(
        functools.partial(kernel, (S, O, limit)),
        out_shape=(
            jax.ShapeDtypeStruct((NJ, SC), F32),
            jax.ShapeDtypeStruct((1, NJ), F32),
            jax.ShapeDtypeStruct((1, SC), F32),
            jax.ShapeDtypeStruct((1, 1), F32),
        ),
        in_specs=[vmem] * 9,
        out_specs=(vmem,) * 4,
        scratch_shapes=[
            pltpu.VMEM((NK, S, B, KC), F32),
            pltpu.VMEM((O, S, 2, SC), F32),
            pltpu.VMEM((D, T // STEM, SC), F32),
            pltpu.VMEM((D, T // STEM, SC), F32),
            pltpu.VMEM((D, STEM, SC), F32),
            pltpu.VMEM((D, STEM, SC), F32),
            pltpu.VMEM((T, SC), F32),
            pltpu.VMEM((R, NJ), BF16),
            pltpu.VMEM((NJ, R), BF16),
            pltpu.VMEM((NJ, 2 * KC), BF16),
            pltpu.VMEM((D, 2 * SL, KC), BF16),
            pltpu.VMEM((D, SL, SC), F32),
            pltpu.VMEM((R, 2 * SC), BF16),
            pltpu.VMEM((NJ, SC), BF16),
            pltpu.VMEM((NJ, SC), BF16),
            pltpu.VMEM((ITERS, 1, NJ + 128), F32),
            pltpu.VMEM((ITERS, S, 1, NJ + 128), F32),
            pltpu.VMEM((ITERS, 1, SC), F32),
            pltpu.VMEM((ITERS, O, 1, SC), F32),
            dma((NK, 2, S)),
            dma((NK, 2, S)),
            dma((NK,)),
            dma,
            dma((S,)),
            dma((S,)),
            dma((O,)),
            dma((O,)),
            dma((ITERS, S)),
            dma((ITERS, S)),
            dma((ITERS, O)),
            dma((ITERS, O)),
        ],
        compiler_params=pltpu.CompilerParams(
            collective_id=0, has_side_effects=True, vmem_limit_bytes=60000 * 1024
        ),
        name="hedge",
    )(
        option_coefs,
        prm_in,
        underlying_of.reshape(S, 1, B),
        underlying_of,
        cost.reshape(1, NJ),
        positions.reshape(1, NJ),
        base_loss.reshape(1, SC),
        duals.reshape(1, SC),
        threshold.reshape(1, 1),
    )
    return (values, x.reshape(NJ), y.reshape(SC), z.reshape(1))


def solution(mesh):
    in_specs = (
        P(("opt", "scen"), None),
        P("opt", None),
        P(("scen", "opt"), None),
        P(("scen", "opt"), None),
        P("opt"),
        P("opt"),
        P("scen"),
        P("scen"),
        P(),
    )
    out_specs = (P("opt", "scen"), P("opt"), P("scen"), P())
    return jax.shard_map(
        on_device, mesh=mesh, in_specs=in_specs, out_specs=out_specs, check_vma=False
    )
```

```python
import functools
import math

import jax
import jax.numpy as jnp
from jax import lax
from jax.experimental import pallas as pl
from jax.experimental.pallas import tpu as pltpu
from jax.sharding import PartitionSpec as P

ITERS = 2

LOW_END = -4.0
HIGH_END = 4.0
TAIL_LEVEL = 0.9
PRIMAL_STEP = 0.5
THRESH_STEP = 0.05
DUAL_STEP = 0.5

MESH = pl.DeviceIdType.MESH
CHUNK = 256
STEM = 64
F32 = jnp.float32
BF16 = jnp.bfloat16


def flip(index, bits):
    out = index
    place = 1
    while place <= bits:
        if bits & place:
            bit = lax.rem(index // place, 2)
            out = out + place * (1 - 2 * bit)
        place *= 2
    return out


def halves(x):
    high = x.astype(BF16)
    low = (x - high.astype(F32)).astype(BF16)
    return high, low


def turn(x):
    x = x - jnp.floor(x + 0.5)
    h = x * math.pi
    z = h * h
    s = F32(-1.0 / 39916800.0)
    for c in (1.0 / 362880.0, -1.0 / 5040.0, 1.0 / 120.0, -1.0 / 6.0, 1.0):
        s = s * z + F32(c)
    s = s * h
    c_ = F32(1.0 / 479001600.0)
    for c in (-1.0 / 3628800.0, 1.0 / 40320.0, -1.0 / 720.0, 1.0 / 24.0, -0.5, 1.0):
        c_ = c_ * z + F32(c)
    return 1.0 - 2.0 * s * s, 2.0 * s * c_


def kernel(
    dims,
    coef, mean_in, spread_in, urow, cost, pos, base, dual, thr,
    val_out, x_out, y_out, z_out,
    F, prm, base_c, base_s, stem_c, stem_s, ksq, Pm, PT, fhl, Fs, acc, ahl, VH, VL,
    gst, gbuf, pst, pbuf,
    ag_send, ag_recv, own_sem, prm_own, pa_send, pa_recv, pb_send, pb_recv,
    g_send, g_recv, p_send, p_recv,
):
    S, O, limit = dims
    D = S * O
    B, T = coef.shape
    SC = base.shape[1]
    NJ = S * B
    SL = S * limit
    R = D * SL
    KC = F.shape[3]
    NK = T // KC
    Q = KC // STEM
    H = B // 2
    n = S.bit_length() - 1
    me = lax.axis_index("scen")
    col = lax.axis_index("opt")

    barrier = pltpu.get_barrier_semaphore()
    for e in range(1, S):
        pl.semaphore_signal(barrier, inc=1, device_id=(flip(me, e), col), device_id_type=MESH)
    for e in range(1, O):
        pl.semaphore_signal(barrier, inc=1, device_id=(me, flip(col, e)), device_id_type=MESH)
    pl.semaphore_wait(barrier, S + O - 2)

    def scenarios(ref, block):
        return ref.at[:, pl.ds(pl.multiple_of(block * SC, SC), SC)]

    def prm_a(e, i):
        peer = flip(me, e)
        return pltpu.make_async_remote_copy(
            src_ref=scenarios((mean_in, spread_in)[i], peer), dst_ref=prm.at[col, me, i],
            send_sem=pa_send.at[e, i], recv_sem=pa_recv.at[e, i],
            device_id=(peer, col), device_id_type=MESH)

    def prm_mine(i):
        return pltpu.make_async_copy(
            scenarios((mean_in, spread_in)[i], me), prm.at[col, me, i], prm_own.at[i])

    def prm_b(e):
        peer = flip(col, e)
        return pltpu.make_async_remote_copy(
            src_ref=prm.at[col], dst_ref=prm.at[col],
            send_sem=pb_send.at[e], recv_sem=pb_recv.at[e],
            device_id=(me, peer), device_id_type=MESH)

    for i in range(2):
        for e in range(1, S):
            prm_a(e, i).start()
        prm_mine(i).start()

    def piece(kc, h, held, d):
        block = flip(me, held)
        rows = pl.ds(h * H, H)
        if held == 0:
            src = coef.at[rows, pl.ds(kc * KC, KC)]
        else:
            src = F.at[kc, block, rows]
        to = held ^ (1 << d)
        return pltpu.make_async_remote_copy(
            src_ref=src, dst_ref=F.at[kc, block, rows],
            send_sem=ag_send.at[kc, h, to], recv_sem=ag_recv.at[kc, h, to],
            device_id=(flip(me, 1 << d), col), device_id_type=MESH)

    def landed(kc, h, e):
        slot = F.at[kc, flip(me, e), pl.ds(h * H, H)]
        pltpu.make_async_remote_copy(
            src_ref=slot, dst_ref=slot,
            send_sem=ag_send.at[kc, h, e], recv_sem=ag_recv.at[kc, h, e],
            device_id=(flip(me, 1), col), device_id_type=MESH).wait_recv()

    orders = [[(h + i) % n for i in range(n)] for h in range(2)]

    def plan(h):
        out = [(0, orders[h])]
        for i, d in enumerate(orders[h]):
            out += [(held ^ (1 << d), orders[h][i + 1:]) for held, _ in list(out)]
        return out

    def own(kc):
        for i in range(n):
            for h in range(2):
                piece(kc, h, 0, orders[h][i]).start()
        pltpu.make_async_copy(
            coef.at[:, pl.ds(kc * KC, KC)], F.at[kc, me], own_sem.at[kc]).start()

    def forward(kc):
        plans = [plan(h) for h in range(2)]
        for i in range(1, S):
            for h in range(2):
                held, later = plans[h][i]
                if later:
                    landed(kc, h, held)
                    for d in later:
                        piece(kc, h, held, d).start()

    def complete(kc):
        for h in range(2):
            for held, later in plan(h)[1:]:
                if not later:
                    landed(kc, h, held)
        pltpu.make_async_copy(
            coef.at[:, pl.ds(kc * KC, KC)], F.at[kc, me], own_sem.at[kc]).wait()

    own(0)
    if NK > 1:
        own(1)

    for i in range(2):
        prm_mine(i).wait()
        for e in range(1, S):
            prm_a(e, i).wait_recv()
    for e in range(1, O):
        prm_b(e).start()

    sub = lax.broadcasted_iota(jnp.int32, (B, B), 0)
    lane = lax.broadcasted_iota(jnp.int32, (B, B), 1)
    for b in range(S):
        ur = urow[b].astype(F32)
        uc = jnp.sum(jnp.where(sub == lane, ur, 0.0), axis=1, keepdims=True)
        same = uc == ur
        rank_r = jnp.sum(jnp.where(same & (sub < lane), 1.0, 0.0), axis=0, keepdims=True)
        rank_c = jnp.sum(jnp.where(same & (lane < sub), 1.0, 0.0), axis=1, keepdims=True)
        place_r = (ur * SL + (rank_r + float(b * limit))).astype(jnp.int32)
        place_c = (uc * SL + (rank_c + float(b * limit))).astype(jnp.int32)
        Pm[:, b * B:(b + 1) * B] = jnp.where(
            lax.broadcasted_iota(jnp.int32, (R, B), 0) == place_r, 1.0, 0.0).astype(BF16)
        PT[b * B:(b + 1) * B, :] = jnp.where(
            lax.broadcasted_iota(jnp.int32, (B, R), 1) == place_c, 1.0, 0.0).astype(BF16)
    term = lax.broadcasted_iota(jnp.int32, (T, SC), 0).astype(F32)
    ksq[...] = term * term

    forward(0)
    if NK > 2:
        own(2)
    for e in range(1, O):
        prm_b(e).wait_recv()

    NB = T // STEM
    idx = lax.broadcasted_iota(jnp.int32, (16 + NB, SC), 0)
    kv = jnp.where(idx < 8, idx, jnp.where(idx == 8, 8, jnp.where(idx == 9, 16, jnp.where(idx == 10, 32, 0))))
    kv = jnp.where(idx >= 16, STEM * (idx - 16), kv).astype(F32)

    def stems(u, carry):
        mean = prm[lax.rem(u, O), u // O, 0]
        x = (mean - LOW_END) * (0.5 / (HIGH_END - LOW_END))
        xh = jnp.floor(x * 4096.0 + 0.5) * (1.0 / 4096.0)
        xl = x - xh
        ph = kv * xh
        ph = ph - jnp.floor(ph + 0.5)
        c, s = turn(ph + kv * xl)
        base_c[u] = c[16:]
        base_s[u] = s[16:]
        cs, ss = c[0:8], s[0:8]
        for i in range(3):
            c1, s1 = c[8 + i:9 + i], s[8 + i:9 + i]
            cs, ss = (jnp.concatenate([cs, cs * c1 - ss * s1], 0),
                      jnp.concatenate([ss, ss * c1 + cs * s1], 0))
        stem_c[u] = cs
        stem_s[u] = ss
        return carry

    lax.fori_loop(0, D, stems, 0, unroll=2)
    if NK > 1:
        forward(1)
    if NK > 3:
        own(3)
    for kc in range(4, NK):
        own(kc)

    RB = 128
    freq2 = -0.5 * (math.pi / (HIGH_END - LOW_END)) ** 2 / math.log(2.0)
    for kc in range(NK):
        complete(kc)
        if kc + 2 < NK:
            forward(kc + 2)
        for b in range(S):
            f = F[kc, b] * (2.0 / (HIGH_END - LOW_END))
            if kc == 0:
                f = jnp.where(lax.broadcasted_iota(jnp.int32, (B, KC), 1) == 0, f * 0.5, f)
            hi, lo = halves(f)
            fhl[b * B:(b + 1) * B, 0:KC] = hi
            fhl[b * B:(b + 1) * B, KC:2 * KC] = lo

        def arrange(r, carry):
            got = jnp.dot(Pm[pl.ds(pl.multiple_of(r * RB, RB), RB), :], fhl[...],
                          preferred_element_type=F32).astype(BF16)
            per = RB // SL
            at = pl.ds(r * per, per)
            Fs[at, 0:SL, :] = got[:, 0:KC].reshape(per, SL, KC)
            Fs[at, SL:2 * SL, :] = got[:, KC:].reshape(per, SL, KC)
            return carry

        lax.fori_loop(0, R // RB, arrange, 0)

        def price(u, carry):
            decay = prm[lax.rem(u, O), u // O, 1] * freq2
            highs, lows = [], []
            for q in range(Q):
                g = kc * Q + q
                c = base_c[u, g:g + 1, :] * stem_c[u] - base_s[u, g:g + 1, :] * stem_s[u]
                v = c * jnp.exp2(decay * ksq[g * STEM:(g + 1) * STEM, :])
                hi, lo = halves(v)
                highs.append(hi)
                lows.append(lo)
            both = jnp.dot(Fs[u], jnp.concatenate(highs, 0), preferred_element_type=F32)
            low = jnp.dot(Fs[u, 0:SL, :], jnp.concatenate(lows, 0), preferred_element_type=F32)
            total = both[0:SL] + (both[SL:] + low)
            acc[u] = total if kc == 0 else acc[u] + total
            return carry

        lax.fori_loop(0, D, price, 0, unroll=4)

    def spread_halves(u, carry):
        hi, lo = halves(acc[u])
        at = pl.ds(pl.multiple_of(u * SL, SL), SL)
        ahl[at, 0:SC] = hi
        ahl[at, SC:2 * SC] = lo
        return carry

    lax.fori_loop(0, D, spread_halves, 0)

    def restore(r, carry):
        at = pl.ds(pl.multiple_of(r * B, B), B)
        got = jnp.dot(PT[at, :], ahl[...], preferred_element_type=F32)
        val_out[at, :] = got[:, 0:SC] + got[:, SC:]
        VH[at, :] = got[:, 0:SC].astype(BF16)
        VL[at, :] = got[:, SC:].astype(BF16)
        return carry

    lax.fori_loop(0, S, restore, 0)

    def pair(row):
        hi = row.astype(BF16).astype(F32)
        at = lax.broadcasted_iota(jnp.int32, (16, row.shape[1]), 0)
        return jnp.where(at == 0, hi, jnp.where(at == 1, row - hi, 0.0)).astype(BF16)

    def product(row, contract):
        lhs = pair(row)
        dn = (((1,), (contract,)), ((), ()))
        out = lax.dot_general(lhs, VH[...], dn, preferred_element_type=F32)
        out = out + lax.dot_general(lhs, VL[...], dn, preferred_element_type=F32)
        return out[0:1] + out[1:2]

    root_scen = math.sqrt(S * SC)
    root_opt = math.sqrt(O * NJ)
    tail = (1.0 - TAIL_LEVEL) * (S * SC)
    x = pos[...]
    y = dual[...]
    z = thr[...]

    def g_copy(it, e):
        return pltpu.make_async_remote_copy(
            src_ref=gst.at[it], dst_ref=gbuf.at[it, me],
            send_sem=g_send.at[it, e], recv_sem=g_recv.at[it, e],
            device_id=(flip(me, e), col), device_id_type=MESH)

    def p_copy(it, e):
        return pltpu.make_async_remote_copy(
            src_ref=pst.at[it], dst_ref=pbuf.at[it, col],
            send_sem=p_send.at[it, e], recv_sem=p_recv.at[it, e],
            device_id=(me, flip(col, e)), device_id_type=MESH)

    for it in range(ITERS):
        part = product(y, 1)
        mass = jnp.broadcast_to(jnp.sum(y, axis=1, keepdims=True), (1, 128))
        gst[it, :, 0:NJ] = part
        gst[it, :, NJ:] = mass
        for e in range(1, S):
            g_copy(it, e).start()
        gbuf[it, me] = gst[it]
        for e in range(1, S):
            g_copy(it, e).wait_recv()
        g = gbuf[it, 0]
        for s in range(1, S):
            g = g + gbuf[it, s]
        x_new = jnp.clip(x - PRIMAL_STEP * (cost[...] - g[:, 0:NJ] / root_scen), -1.0, 1.0)
        z_new = z - THRESH_STEP * (1.0 - g[:, NJ:NJ + 1] / tail)
        x_bar = 2.0 * x_new - x
        z_bar = 2.0 * z_new - z
        pst[it] = product(x_bar, 0)
        for e in range(1, O):
            p_copy(it, e).start()
        pbuf[it, col] = pst[it]
        for e in range(1, O):
            p_copy(it, e).wait_recv()
        p = pbuf[it, 0]
        for o in range(1, O):
            p = p + pbuf[it, o]
        y = jnp.clip(y + DUAL_STEP * (base[...] - p / root_opt - z_bar), 0.0, 1.0)
        x, z = x_new, z_new
    x_out[...] = x
    y_out[...] = y
    z_out[...] = z

    for e in range(1, S):
        for i in range(2):
            prm_a(e, i).wait_send()
    for e in range(1, O):
        prm_b(e).wait_send()
    for kc in range(NK):
        for h in range(2):
            for held, later in plan(h):
                for d in later:
                    piece(kc, h, held, d).wait_send()
    for it in range(ITERS):
        for e in range(1, S):
            g_copy(it, e).wait_send()
        for e in range(1, O):
            p_copy(it, e).wait_send()


def on_device(
    option_coefs,
    underlying_of,
    log_return_mean,
    log_return_spread,
    cost,
    positions,
    base_loss,
    duals,
    threshold,
):
    S = lax.axis_size("scen")
    O = lax.axis_size("opt")
    D = S * O
    B, T = option_coefs.shape
    SC = duals.shape[0]
    NJ = S * B
    limit = max(2, 2 * B // D)
    SL = S * limit
    R = D * SL
    KC = min(CHUNK, T)
    NK = T // KC
    vmem = pl.BlockSpec(memory_space=pltpu.VMEM)
    dma = pltpu.SemaphoreType.DMA
    values, x, y, z = pl.pallas_call(
        functools.partial(kernel, (S, O, limit)),
        out_shape=(
            jax.ShapeDtypeStruct((NJ, SC), F32),
            jax.ShapeDtypeStruct((1, NJ), F32),
            jax.ShapeDtypeStruct((1, SC), F32),
            jax.ShapeDtypeStruct((1, 1), F32),
        ),
        in_specs=[pl.BlockSpec(memory_space=pl.ANY)] + [vmem] * 8,
        out_specs=(vmem,) * 4,
        scratch_shapes=[
            pltpu.VMEM((NK, S, B, KC), F32),
            pltpu.VMEM((O, S, 2, 1, SC), F32),
            pltpu.VMEM((D, T // STEM, SC), F32),
            pltpu.VMEM((D, T // STEM, SC), F32),
            pltpu.VMEM((D, STEM, SC), F32),
            pltpu.VMEM((D, STEM, SC), F32),
            pltpu.VMEM((T, SC), F32),
            pltpu.VMEM((R, NJ), BF16),
            pltpu.VMEM((NJ, R), BF16),
            pltpu.VMEM((NJ, 2 * KC), BF16),
            pltpu.VMEM((D, 2 * SL, KC), BF16),
            pltpu.VMEM((D, SL, SC), F32),
            pltpu.VMEM((R, 2 * SC), BF16),
            pltpu.VMEM((NJ, SC), BF16),
            pltpu.VMEM((NJ, SC), BF16),
            pltpu.VMEM((ITERS, 1, NJ + 128), F32),
            pltpu.VMEM((ITERS, S, 1, NJ + 128), F32),
            pltpu.VMEM((ITERS, 1, SC), F32),
            pltpu.VMEM((ITERS, O, 1, SC), F32),
            dma((NK, 2, S)),
            dma((NK, 2, S)),
            dma((NK,)),
            dma((2,)),
            dma((S, 2)),
            dma((S, 2)),
            dma((O,)),
            dma((O,)),
            dma((ITERS, S)),
            dma((ITERS, S)),
            dma((ITERS, O)),
            dma((ITERS, O)),
        ],
        compiler_params=pltpu.CompilerParams(
            collective_id=0, has_side_effects=True, vmem_limit_bytes=60000 * 1024
        ),
        name="hedge",
    )(
        option_coefs,
        log_return_mean,
        log_return_spread,
        underlying_of.reshape(S, 1, B),
        cost.reshape(1, NJ),
        positions.reshape(1, NJ),
        base_loss.reshape(1, SC),
        duals.reshape(1, SC),
        threshold.reshape(1, 1),
    )
    return (values, x.reshape(NJ), y.reshape(SC), z.reshape(1))


def solution(mesh):
    in_specs = (
        P(("opt", "scen"), None),
        P("opt", None),
        P(("scen", "opt"), None),
        P(("scen", "opt"), None),
        P("opt"),
        P("opt"),
        P("scen"),
        P("scen"),
        P(),
    )
    out_specs = (P("opt", "scen"), P("opt"), P("scen"), P())
    return jax.shard_map(
        on_device, mesh=mesh, in_specs=in_specs, out_specs=out_specs, check_vma=False
    )
```

```python
import functools
import math

import jax
import jax.numpy as jnp
from jax import lax
from jax.experimental import pallas as pl
from jax.experimental.pallas import tpu as pltpu
from jax.sharding import PartitionSpec as P

ITERS = 2

LOW_END = -4.0
HIGH_END = 4.0
TAIL_LEVEL = 0.9
PRIMAL_STEP = 0.5
THRESH_STEP = 0.05
DUAL_STEP = 0.5

MESH = pl.DeviceIdType.MESH
CHUNK = 256
F32 = jnp.float32
BF16 = jnp.bfloat16


def flip(index, bits):
    out = index
    place = 1
    while place <= bits:
        if bits & place:
            bit = lax.rem(index // place, 2)
            out = out + place * (1 - 2 * bit)
        place *= 2
    return out


def halves(x):
    high = x.astype(BF16)
    low = (x - high.astype(F32)).astype(BF16)
    return high, low


def turn(x):
    x = x - jnp.floor(x + 0.5)
    h = x * math.pi
    z = h * h
    s = F32(-1.0 / 39916800.0)
    for c in (1.0 / 362880.0, -1.0 / 5040.0, 1.0 / 120.0, -1.0 / 6.0, 1.0):
        s = s * z + F32(c)
    s = s * h
    c_ = F32(1.0 / 479001600.0)
    for c in (-1.0 / 3628800.0, 1.0 / 40320.0, -1.0 / 720.0, 1.0 / 24.0, -0.5, 1.0):
        c_ = c_ * z + F32(c)
    return 1.0 - 2.0 * s * s, 2.0 * s * c_


def kernel(
    dims,
    coef, mean_in, spread_in, urow, cost, pos, base, dual, thr,
    VH, VL, x_out, y_out, z_out,
    F, prm, mid_c, mid_s, off_c, off_s, ksq, Pm, PT, fhl, Fs, acc, ahl,
    gst, gbuf, pst, pbuf,
    ag_send, ag_recv, own_sem, prm_own, pa_send, pa_recv, pb_send, pb_recv,
    g_send, g_recv, p_send, p_recv,
):
    S, O, limit = dims
    D = S * O
    B, T = coef.shape
    SC = base.shape[1]
    NJ = S * B
    SL = S * limit
    R = D * SL
    KC = F.shape[3]
    NK = T // KC
    M = KC // 16
    H = B // 2
    n = S.bit_length() - 1
    me = lax.axis_index("scen")
    col = lax.axis_index("opt")

    barrier = pltpu.get_barrier_semaphore()
    for e in range(1, S):
        pl.semaphore_signal(barrier, inc=1, device_id=(flip(me, e), col), device_id_type=MESH)
    for e in range(1, O):
        pl.semaphore_signal(barrier, inc=1, device_id=(me, flip(col, e)), device_id_type=MESH)
    pl.semaphore_wait(barrier, S + O - 2)

    def scenarios(ref, block):
        return ref.at[:, pl.ds(pl.multiple_of(block * SC, SC), SC)]

    def prm_a(e, i):
        peer = flip(me, e)
        return pltpu.make_async_remote_copy(
            src_ref=scenarios((mean_in, spread_in)[i], peer), dst_ref=prm.at[col, me, i],
            send_sem=pa_send.at[e, i], recv_sem=pa_recv.at[e, i],
            device_id=(peer, col), device_id_type=MESH)

    def prm_mine(i):
        return pltpu.make_async_copy(
            scenarios((mean_in, spread_in)[i], me), prm.at[col, me, i], prm_own.at[i])

    def prm_b(e):
        peer = flip(col, e)
        return pltpu.make_async_remote_copy(
            src_ref=prm.at[col], dst_ref=prm.at[col],
            send_sem=pb_send.at[e], recv_sem=pb_recv.at[e],
            device_id=(me, peer), device_id_type=MESH)

    for i in range(2):
        for e in range(1, S):
            prm_a(e, i).start()
        prm_mine(i).start()

    def piece(kc, h, held, d):
        block = flip(me, held)
        rows = pl.ds(h * H, H)
        if held == 0:
            src = coef.at[rows, pl.ds(kc * KC, KC)]
        else:
            src = F.at[kc, block, rows]
        to = held ^ (1 << d)
        return pltpu.make_async_remote_copy(
            src_ref=src, dst_ref=F.at[kc, block, rows],
            send_sem=ag_send.at[kc, h, to], recv_sem=ag_recv.at[kc, h, to],
            device_id=(flip(me, 1 << d), col), device_id_type=MESH)

    def landed(kc, h, e):
        slot = F.at[kc, flip(me, e), pl.ds(h * H, H)]
        pltpu.make_async_remote_copy(
            src_ref=slot, dst_ref=slot,
            send_sem=ag_send.at[kc, h, e], recv_sem=ag_recv.at[kc, h, e],
            device_id=(flip(me, 1), col), device_id_type=MESH).wait_recv()

    orders = [[(h + i) % n for i in range(n)] for h in range(2)]

    def plan(h):
        out = [(0, orders[h])]
        for i, d in enumerate(orders[h]):
            out += [(held ^ (1 << d), orders[h][i + 1:]) for held, _ in list(out)]
        return out

    def own(kc):
        for i in range(n):
            for h in range(2):
                piece(kc, h, 0, orders[h][i]).start()
        pltpu.make_async_copy(
            coef.at[:, pl.ds(kc * KC, KC)], F.at[kc, me], own_sem.at[kc]).start()

    def forward(kc):
        plans = [plan(h) for h in range(2)]
        for i in range(1, S):
            for h in range(2):
                held, later = plans[h][i]
                if later:
                    landed(kc, h, held)
                    for d in later:
                        piece(kc, h, held, d).start()

    def complete(kc):
        for h in range(2):
            for held, later in plan(h)[1:]:
                if not later:
                    landed(kc, h, held)
        pltpu.make_async_copy(
            coef.at[:, pl.ds(kc * KC, KC)], F.at[kc, me], own_sem.at[kc]).wait()

    own(0)
    if NK > 1:
        own(1)

    for i in range(2):
        prm_mine(i).wait()
        for e in range(1, S):
            prm_a(e, i).wait_recv()
    for e in range(1, O):
        prm_b(e).start()

    sub = lax.broadcasted_iota(jnp.int32, (B, B), 0)
    lane = lax.broadcasted_iota(jnp.int32, (B, B), 1)
    for b in range(S):
        ur = urow[b].astype(F32)
        uc = jnp.sum(jnp.where(sub == lane, ur, 0.0), axis=1, keepdims=True)
        same = uc == ur
        rank_r = jnp.sum(jnp.where(same & (sub < lane), 1.0, 0.0), axis=0, keepdims=True)
        rank_c = jnp.sum(jnp.where(same & (lane < sub), 1.0, 0.0), axis=1, keepdims=True)
        place_r = (ur * SL + (rank_r + float(b * limit))).astype(jnp.int32)
        place_c = (uc * SL + (rank_c + float(b * limit))).astype(jnp.int32)
        Pm[:, b * B:(b + 1) * B] = jnp.where(
            lax.broadcasted_iota(jnp.int32, (R, B), 0) == place_r, 1.0, 0.0).astype(BF16)
        PT[b * B:(b + 1) * B, :] = jnp.where(
            lax.broadcasted_iota(jnp.int32, (B, R), 1) == place_c, 1.0, 0.0).astype(BF16)
    term = lax.broadcasted_iota(jnp.int32, (T, SC), 0).astype(F32)
    ksq[...] = term * term

    forward(0)
    if NK > 2:
        own(2)
    for e in range(1, O):
        prm_b(e).wait_recv()

    idx = lax.broadcasted_iota(jnp.int32, (8 * NK + M, SC), 0)
    kv = jnp.where(idx < 8 * NK, (idx // 8) * KC + (KC // 2 - 4) + lax.rem(idx, 8),
                   8 * (idx - 8 * NK) + 4).astype(F32)

    def stems(u, carry):
        mean = prm[lax.rem(u, O), u // O, 0]
        x = (mean - LOW_END) * (0.5 / (HIGH_END - LOW_END))
        xh = jnp.floor(x * 4096.0 + 0.5) * (1.0 / 4096.0)
        xl = x - xh
        ph = kv * xh
        ph = ph - jnp.floor(ph + 0.5)
        c, s = turn(ph + kv * xl)
        mid_c[u] = c[0:8 * NK]
        mid_s[u] = s[0:8 * NK]
        off_c[u] = c[8 * NK:]
        off_s[u] = s[8 * NK:]
        return carry

    lax.fori_loop(0, D, stems, 0, unroll=2)
    if NK > 1:
        forward(1)
    if NK > 3:
        own(3)
    for kc in range(4, NK):
        own(kc)

    RB = 128
    freq2 = -0.5 * (math.pi / (HIGH_END - LOW_END)) ** 2 / math.log(2.0)
    for kc in range(NK):
        complete(kc)
        if kc + 2 < NK:
            forward(kc + 2)
        for b in range(S):
            f = F[kc, b] * (2.0 / (HIGH_END - LOW_END))
            if kc == 0:
                f = jnp.where(lax.broadcasted_iota(jnp.int32, (B, KC), 1) == 0, f * 0.5, f)
            hi, lo = halves(f)
            fhl[b * B:(b + 1) * B, 0:KC] = hi
            fhl[b * B:(b + 1) * B, KC:2 * KC] = lo

        def arrange(r, carry):
            got = jnp.dot(Pm[pl.ds(pl.multiple_of(r * RB, RB), RB), :], fhl[...],
                          preferred_element_type=F32).astype(BF16)
            per = RB // SL
            at = pl.ds(r * per, per)
            Fs[at, 0:SL, :] = got[:, 0:KC].reshape(per, SL, KC)
            Fs[at, SL:2 * SL, :] = got[:, KC:].reshape(per, SL, KC)
            return carry

        lax.fori_loop(0, R // RB, arrange, 0)

        def price(u, carry):
            decay = prm[lax.rem(u, O), u // O, 1] * freq2
            mc = mid_c[u, kc * 8:kc * 8 + 8, :]
            ms = mid_s[u, kc * 8:kc * 8 + 8, :]
            highs, lows = [None] * M, [None] * M

            def damped(c, i):
                at = kc * KC + 8 * i
                return c * jnp.exp2(decay * ksq[at:at + 8, :])

            for m in range(0, M, 2):
                a0, b0 = mc * off_c[u, m:m + 1, :], ms * off_s[u, m:m + 1, :]
                a1, b1 = mc * off_c[u, m + 1:m + 2, :], ms * off_s[u, m + 1:m + 2, :]
                up = (M + m) // 2
                down = (M - 2 - m) // 2
                highs[up], lows[up] = halves(jnp.concatenate(
                    [damped(a0 - b0, M + m), damped(a1 - b1, M + m + 1)], 0))
                highs[down], lows[down] = halves(jnp.concatenate(
                    [damped(a1 + b1, M - 2 - m), damped(a0 + b0, M - 1 - m)], 0))
            both = jnp.dot(Fs[u], jnp.concatenate(highs, 0), preferred_element_type=F32)
            low = jnp.dot(Fs[u, 0:SL, :], jnp.concatenate(lows, 0), preferred_element_type=F32)
            total = both[0:SL] + (both[SL:] + low)
            acc[u] = total if kc == 0 else acc[u] + total
            return carry

        lax.fori_loop(0, D, price, 0, unroll=4)

    def spread_halves(u, carry):
        hi, lo = halves(acc[u])
        at = pl.ds(pl.multiple_of(u * SL, SL), SL)
        ahl[at, 0:SC] = hi
        ahl[at, SC:2 * SC] = lo
        return carry

    lax.fori_loop(0, D, spread_halves, 0)

    def restore(r, carry):
        at = pl.ds(pl.multiple_of(r * B, B), B)
        got = jnp.dot(PT[at, :], ahl[...], preferred_element_type=F32)
        VH[at, :] = got[:, 0:SC].astype(BF16)
        VL[at, :] = got[:, SC:].astype(BF16)
        return carry

    lax.fori_loop(0, S, restore, 0)

    def pair(row):
        hi = row.astype(BF16).astype(F32)
        at = lax.broadcasted_iota(jnp.int32, (16, row.shape[1]), 0)
        return jnp.where(at == 0, hi, jnp.where(at == 1, row - hi, 0.0)).astype(BF16)

    def product(row, contract):
        lhs = pair(row)
        dn = (((1,), (contract,)), ((), ()))
        out = lax.dot_general(lhs, VH[...], dn, preferred_element_type=F32)
        out = out + lax.dot_general(lhs, VL[...], dn, preferred_element_type=F32)
        return out[0:1] + out[1:2]

    root_scen = math.sqrt(S * SC)
    root_opt = math.sqrt(O * NJ)
    tail = (1.0 - TAIL_LEVEL) * (S * SC)
    x = pos[...]
    y = dual[...]
    z = thr[...]

    def g_copy(it, e):
        return pltpu.make_async_remote_copy(
            src_ref=gst.at[it], dst_ref=gbuf.at[it, me],
            send_sem=g_send.at[it, e], recv_sem=g_recv.at[it, e],
            device_id=(flip(me, e), col), device_id_type=MESH)

    def p_copy(it, e):
        return pltpu.make_async_remote_copy(
            src_ref=pst.at[it], dst_ref=pbuf.at[it, col],
            send_sem=p_send.at[it, e], recv_sem=p_recv.at[it, e],
            device_id=(me, flip(col, e)), device_id_type=MESH)

    for it in range(ITERS):
        part = product(y, 1)
        mass = jnp.broadcast_to(jnp.sum(y, axis=1, keepdims=True), (1, 128))
        gst[it, :, 0:NJ] = part
        gst[it, :, NJ:] = mass
        for e in range(1, S):
            g_copy(it, e).start()
        gbuf[it, me] = gst[it]
        for e in range(1, S):
            g_copy(it, e).wait_recv()
        g = gbuf[it, 0]
        for s in range(1, S):
            g = g + gbuf[it, s]
        x_new = jnp.clip(x - PRIMAL_STEP * (cost[...] - g[:, 0:NJ] / root_scen), -1.0, 1.0)
        z_new = z - THRESH_STEP * (1.0 - g[:, NJ:NJ + 1] / tail)
        x_bar = 2.0 * x_new - x
        z_bar = 2.0 * z_new - z
        pst[it] = product(x_bar, 0)
        for e in range(1, O):
            p_copy(it, e).start()
        pbuf[it, col] = pst[it]
        for e in range(1, O):
            p_copy(it, e).wait_recv()
        p = pbuf[it, 0]
        for o in range(1, O):
            p = p + pbuf[it, o]
        y = jnp.clip(y + DUAL_STEP * (base[...] - p / root_opt - z_bar), 0.0, 1.0)
        x, z = x_new, z_new
    x_out[...] = x
    y_out[...] = y
    z_out[...] = z

    for e in range(1, S):
        for i in range(2):
            prm_a(e, i).wait_send()
    for e in range(1, O):
        prm_b(e).wait_send()
    for kc in range(NK):
        for h in range(2):
            for held, later in plan(h):
                for d in later:
                    piece(kc, h, held, d).wait_send()
    for it in range(ITERS):
        for e in range(1, S):
            g_copy(it, e).wait_send()
        for e in range(1, O):
            p_copy(it, e).wait_send()


def on_device(
    option_coefs,
    underlying_of,
    log_return_mean,
    log_return_spread,
    cost,
    positions,
    base_loss,
    duals,
    threshold,
):
    S = lax.axis_size("scen")
    O = lax.axis_size("opt")
    D = S * O
    B, T = option_coefs.shape
    SC = duals.shape[0]
    NJ = S * B
    limit = max(2, 2 * B // D)
    SL = S * limit
    R = D * SL
    KC = min(CHUNK, T)
    NK = T // KC
    vmem = pl.BlockSpec(memory_space=pltpu.VMEM)
    dma = pltpu.SemaphoreType.DMA
    high, low, x, y, z = pl.pallas_call(
        functools.partial(kernel, (S, O, limit)),
        out_shape=(
            jax.ShapeDtypeStruct((NJ, SC), BF16),
            jax.ShapeDtypeStruct((NJ, SC), BF16),
            jax.ShapeDtypeStruct((1, NJ), F32),
            jax.ShapeDtypeStruct((1, SC), F32),
            jax.ShapeDtypeStruct((1, 1), F32),
        ),
        in_specs=[pl.BlockSpec(memory_space=pl.ANY)] + [vmem] * 8,
        out_specs=(vmem,) * 5,
        scratch_shapes=[
            pltpu.VMEM((NK, S, B, KC), F32),
            pltpu.VMEM((O, S, 2, 1, SC), F32),
            pltpu.VMEM((D, 8 * NK, SC), F32),
            pltpu.VMEM((D, 8 * NK, SC), F32),
            pltpu.VMEM((D, KC // 16, SC), F32),
            pltpu.VMEM((D, KC // 16, SC), F32),
            pltpu.VMEM((T, SC), F32),
            pltpu.VMEM((R, NJ), BF16),
            pltpu.VMEM((NJ, R), BF16),
            pltpu.VMEM((NJ, 2 * KC), BF16),
            pltpu.VMEM((D, 2 * SL, KC), BF16),
            pltpu.VMEM((D, SL, SC), F32),
            pltpu.VMEM((R, 2 * SC), BF16),
            pltpu.VMEM((ITERS, 1, NJ + 128), F32),
            pltpu.VMEM((ITERS, S, 1, NJ + 128), F32),
            pltpu.VMEM((ITERS, 1, SC), F32),
            pltpu.VMEM((ITERS, O, 1, SC), F32),
            dma((NK, 2, S)),
            dma((NK, 2, S)),
            dma((NK,)),
            dma((2,)),
            dma((S, 2)),
            dma((S, 2)),
            dma((O,)),
            dma((O,)),
            dma((ITERS, S)),
            dma((ITERS, S)),
            dma((ITERS, O)),
            dma((ITERS, O)),
        ],
        compiler_params=pltpu.CompilerParams(
            collective_id=0, has_side_effects=True, vmem_limit_bytes=60000 * 1024
        ),
        name="hedge",
    )(
        option_coefs,
        log_return_mean,
        log_return_spread,
        underlying_of.reshape(S, 1, B),
        cost.reshape(1, NJ),
        positions.reshape(1, NJ),
        base_loss.reshape(1, SC),
        duals.reshape(1, SC),
        threshold.reshape(1, 1),
    )
    values = high.astype(F32) + low.astype(F32)
    return (values, x.reshape(NJ), y.reshape(SC), z.reshape(1))


def solution(mesh):
    in_specs = (
        P(("opt", "scen"), None),
        P("opt", None),
        P(("scen", "opt"), None),
        P(("scen", "opt"), None),
        P("opt"),
        P("opt"),
        P("scen"),
        P("scen"),
        P(),
    )
    out_specs = (P("opt", "scen"), P("opt"), P("scen"), P())
    return jax.shard_map(
        on_device, mesh=mesh, in_specs=in_specs, out_specs=out_specs, check_vma=False
    )
```

```python
import functools
import math

import jax
import jax.numpy as jnp
from jax import lax
from jax.experimental import pallas as pl
from jax.experimental.pallas import tpu as pltpu
from jax.sharding import PartitionSpec as P

ITERS = 2

LOW_END = -4.0
HIGH_END = 4.0
TAIL_LEVEL = 0.9
PRIMAL_STEP = 0.5
THRESH_STEP = 0.05
DUAL_STEP = 0.5

MESH = pl.DeviceIdType.MESH
CHUNK = 256
F32 = jnp.float32
BF16 = jnp.bfloat16


def flip(index, bits):
    out = index
    place = 1
    while place <= bits:
        if bits & place:
            bit = lax.rem(index // place, 2)
            out = out + place * (1 - 2 * bit)
        place *= 2
    return out


def halves(x):
    high = x.astype(BF16)
    low = (x - high.astype(F32)).astype(BF16)
    return high, low


def turn(x):
    x = x - jnp.floor(x + 0.5)
    h = x * math.pi
    z = h * h
    s = F32(-1.0 / 39916800.0)
    for c in (1.0 / 362880.0, -1.0 / 5040.0, 1.0 / 120.0, -1.0 / 6.0, 1.0):
        s = s * z + F32(c)
    s = s * h
    c_ = F32(1.0 / 479001600.0)
    for c in (-1.0 / 3628800.0, 1.0 / 40320.0, -1.0 / 720.0, 1.0 / 24.0, -0.5, 1.0):
        c_ = c_ * z + F32(c)
    return 1.0 - 2.0 * s * s, 2.0 * s * c_


def kernel(
    dims,
    coef, mean_in, spread_in, urow, cost, pos, base, dual, thr,
    VH, VL, x_out, y_out, z_out,
    F, prm, mid_c, mid_s, off_c, off_s, ksq, Pm, PT, fhl, Fs, acc, ahl,
    gst, gbuf, pst, pbuf,
    ag_send, ag_recv, own_sem, prm_own, pa_send, pa_recv, pb_send, pb_recv,
    g_send, g_recv, p_send, p_recv,
):
    S, O, limit = dims
    D = S * O
    B, T = coef.shape
    SC = base.shape[1]
    NJ = S * B
    SL = S * limit
    R = D * SL
    KC = F.shape[3]
    NK = T // KC
    M = KC // 16
    H = B // 2
    n = S.bit_length() - 1
    me = lax.axis_index("scen")
    col = lax.axis_index("opt")

    barrier = pltpu.get_barrier_semaphore()
    for e in range(1, S):
        pl.semaphore_signal(barrier, inc=1, device_id=(flip(me, e), col), device_id_type=MESH)
    for e in range(1, O):
        pl.semaphore_signal(barrier, inc=1, device_id=(me, flip(col, e)), device_id_type=MESH)

    sub = lax.broadcasted_iota(jnp.int32, (B, B), 0)
    lane = lax.broadcasted_iota(jnp.int32, (B, B), 1)
    def sorters(first, last):
        for b in range(first, last):
            ur = urow[b].astype(F32)
            uc = jnp.sum(jnp.where(sub == lane, ur, 0.0), axis=1, keepdims=True)
            same = uc == ur
            rank_r = jnp.sum(jnp.where(same & (sub < lane), 1.0, 0.0), axis=0, keepdims=True)
            rank_c = jnp.sum(jnp.where(same & (lane < sub), 1.0, 0.0), axis=1, keepdims=True)
            place_r = (ur * SL + (rank_r + float(b * limit))).astype(jnp.int32)
            place_c = (uc * SL + (rank_c + float(b * limit))).astype(jnp.int32)
            Pm[:, b * B:(b + 1) * B] = jnp.where(
                lax.broadcasted_iota(jnp.int32, (R, B), 0) == place_r, 1.0, 0.0).astype(BF16)
            PT[b * B:(b + 1) * B, :] = jnp.where(
                lax.broadcasted_iota(jnp.int32, (B, R), 1) == place_c, 1.0, 0.0).astype(BF16)

    sorters(0, S // 2)
    pl.semaphore_wait(barrier, S + O - 2)

    def scenarios(ref, block):
        return ref.at[:, pl.ds(pl.multiple_of(block * SC, SC), SC)]

    def prm_a(e, i):
        peer = flip(me, e)
        return pltpu.make_async_remote_copy(
            src_ref=scenarios((mean_in, spread_in)[i], peer), dst_ref=prm.at[col, me, i],
            send_sem=pa_send.at[e, i], recv_sem=pa_recv.at[e, i],
            device_id=(peer, col), device_id_type=MESH)

    def prm_mine(i):
        return pltpu.make_async_copy(
            scenarios((mean_in, spread_in)[i], me), prm.at[col, me, i], prm_own.at[i])

    def prm_b(e):
        peer = flip(col, e)
        return pltpu.make_async_remote_copy(
            src_ref=prm.at[col], dst_ref=prm.at[col],
            send_sem=pb_send.at[e], recv_sem=pb_recv.at[e],
            device_id=(me, peer), device_id_type=MESH)

    for i in range(2):
        for e in range(1, S):
            prm_a(e, i).start()
        prm_mine(i).start()

    def piece(kc, h, held, d):
        block = flip(me, held)
        rows = pl.ds(h * H, H)
        if held == 0:
            src = coef.at[rows, pl.ds(kc * KC, KC)]
        else:
            src = F.at[kc, block, rows]
        to = held ^ (1 << d)
        return pltpu.make_async_remote_copy(
            src_ref=src, dst_ref=F.at[kc, block, rows],
            send_sem=ag_send.at[kc, h, to], recv_sem=ag_recv.at[kc, h, to],
            device_id=(flip(me, 1 << d), col), device_id_type=MESH)

    def landed(kc, h, e):
        slot = F.at[kc, flip(me, e), pl.ds(h * H, H)]
        pltpu.make_async_remote_copy(
            src_ref=slot, dst_ref=slot,
            send_sem=ag_send.at[kc, h, e], recv_sem=ag_recv.at[kc, h, e],
            device_id=(flip(me, 1), col), device_id_type=MESH).wait_recv()

    orders = [[(h + i) % n for i in range(n)] for h in range(2)]

    def plan(h):
        out = [(0, orders[h])]
        for i, d in enumerate(orders[h]):
            out += [(held ^ (1 << d), orders[h][i + 1:]) for held, _ in list(out)]
        return out

    def own(kc):
        for i in range(n):
            for h in range(2):
                piece(kc, h, 0, orders[h][i]).start()
        pltpu.make_async_copy(
            coef.at[:, pl.ds(kc * KC, KC)], F.at[kc, me], own_sem.at[kc]).start()

    def forward(kc):
        plans = [plan(h) for h in range(2)]
        for i in range(1, S):
            for h in range(2):
                held, later = plans[h][i]
                if later:
                    landed(kc, h, held)
                    for d in later:
                        piece(kc, h, held, d).start()

    def complete(kc):
        for h in range(2):
            for held, later in plan(h)[1:]:
                if not later:
                    landed(kc, h, held)
        pltpu.make_async_copy(
            coef.at[:, pl.ds(kc * KC, KC)], F.at[kc, me], own_sem.at[kc]).wait()

    own(0)
    if NK > 1:
        own(1)

    sorters(S // 2, 3 * S // 4)
    for i in range(2):
        prm_mine(i).wait()
        for e in range(1, S):
            prm_a(e, i).wait_recv()
    for e in range(1, O):
        prm_b(e).start()

    sorters(3 * S // 4, S)
    term = lax.broadcasted_iota(jnp.int32, (T, SC), 0).astype(F32)
    ksq[...] = term * term

    forward(0)
    if NK > 2:
        own(2)
    for e in range(1, O):
        prm_b(e).wait_recv()

    idx = lax.broadcasted_iota(jnp.int32, (8 * NK + M, SC), 0)
    kv = jnp.where(idx < 8 * NK, (idx // 8) * KC + (KC // 2 - 4) + lax.rem(idx, 8),
                   8 * (idx - 8 * NK) + 4).astype(F32)

    def stems(u, carry):
        mean = prm[lax.rem(u, O), u // O, 0]
        x = (mean - LOW_END) * (0.5 / (HIGH_END - LOW_END))
        xh = jnp.floor(x * 4096.0 + 0.5) * (1.0 / 4096.0)
        xl = x - xh
        ph = kv * xh
        ph = ph - jnp.floor(ph + 0.5)
        c, s = turn(ph + kv * xl)
        mid_c[u] = c[0:8 * NK]
        mid_s[u] = s[0:8 * NK]
        off_c[u] = c[8 * NK:]
        off_s[u] = s[8 * NK:]
        return carry

    lax.fori_loop(0, D, stems, 0, unroll=2)
    if NK > 1:
        forward(1)
    if NK > 3:
        own(3)
    for kc in range(4, NK):
        own(kc)

    RB = 128
    freq2 = -0.5 * (math.pi / (HIGH_END - LOW_END)) ** 2 / math.log(2.0)
    for kc in range(NK):
        complete(kc)
        if kc + 2 < NK:
            forward(kc + 2)
        for b in range(S):
            f = F[kc, b] * (2.0 / (HIGH_END - LOW_END))
            if kc == 0:
                f = jnp.where(lax.broadcasted_iota(jnp.int32, (B, KC), 1) == 0, f * 0.5, f)
            hi, lo = halves(f)
            fhl[b * B:(b + 1) * B, 0:KC] = hi
            fhl[b * B:(b + 1) * B, KC:2 * KC] = lo

        def arrange(r, carry):
            got = jnp.dot(Pm[pl.ds(pl.multiple_of(r * RB, RB), RB), :], fhl[...],
                          preferred_element_type=F32).astype(BF16)
            per = RB // SL
            at = pl.ds(r * per, per)
            Fs[at, 0:SL, :] = got[:, 0:KC].reshape(per, SL, KC)
            Fs[at, SL:2 * SL, :] = got[:, KC:].reshape(per, SL, KC)
            return carry

        lax.fori_loop(0, R // RB, arrange, 0)

        def price(u, carry):
            decay = prm[lax.rem(u, O), u // O, 1] * freq2
            mc = mid_c[u, kc * 8:kc * 8 + 8, :]
            ms = mid_s[u, kc * 8:kc * 8 + 8, :]
            highs, lows = [None] * M, [None] * M

            def damped(c, i):
                at = kc * KC + 8 * i
                return c * jnp.exp2(decay * ksq[at:at + 8, :])

            for m in range(0, M, 2):
                a0, b0 = mc * off_c[u, m:m + 1, :], ms * off_s[u, m:m + 1, :]
                a1, b1 = mc * off_c[u, m + 1:m + 2, :], ms * off_s[u, m + 1:m + 2, :]
                up = (M + m) // 2
                down = (M - 2 - m) // 2
                highs[up], lows[up] = halves(jnp.concatenate(
                    [damped(a0 - b0, M + m), damped(a1 - b1, M + m + 1)], 0))
                highs[down], lows[down] = halves(jnp.concatenate(
                    [damped(a1 + b1, M - 2 - m), damped(a0 + b0, M - 1 - m)], 0))
            both = jnp.dot(Fs[u], jnp.concatenate(highs, 0), preferred_element_type=F32)
            low = jnp.dot(Fs[u, 0:SL, :], jnp.concatenate(lows, 0), preferred_element_type=F32)
            total = both[0:SL] + (both[SL:] + low)
            acc[u] = total if kc == 0 else acc[u] + total
            return carry

        lax.fori_loop(0, D, price, 0, unroll=4)

    def spread_halves(u, carry):
        hi, lo = halves(acc[u])
        at = pl.ds(pl.multiple_of(u * SL, SL), SL)
        ahl[at, 0:SC] = hi
        ahl[at, SC:2 * SC] = lo
        return carry

    lax.fori_loop(0, D, spread_halves, 0)

    def restore(r, carry):
        at = pl.ds(pl.multiple_of(r * B, B), B)
        got = jnp.dot(PT[at, :], ahl[...], preferred_element_type=F32)
        VH[at, :] = got[:, 0:SC].astype(BF16)
        VL[at, :] = got[:, SC:].astype(BF16)
        return carry

    lax.fori_loop(0, S, restore, 0)

    def pair(row):
        hi = row.astype(BF16).astype(F32)
        at = lax.broadcasted_iota(jnp.int32, (16, row.shape[1]), 0)
        return jnp.where(at == 0, hi, jnp.where(at == 1, row - hi, 0.0)).astype(BF16)

    def product(row, contract):
        lhs = pair(row)
        dn = (((1,), (contract,)), ((), ()))
        out = lax.dot_general(lhs, VH[...], dn, preferred_element_type=F32)
        out = out + lax.dot_general(lhs, VL[...], dn, preferred_element_type=F32)
        return out[0:1] + out[1:2]

    root_scen = math.sqrt(S * SC)
    root_opt = math.sqrt(O * NJ)
    tail = (1.0 - TAIL_LEVEL) * (S * SC)
    x = pos[...]
    y = dual[...]
    z = thr[...]

    def g_copy(it, e):
        return pltpu.make_async_remote_copy(
            src_ref=gst.at[it], dst_ref=gbuf.at[it, me],
            send_sem=g_send.at[it, e], recv_sem=g_recv.at[it, e],
            device_id=(flip(me, e), col), device_id_type=MESH)

    def p_copy(it, e):
        return pltpu.make_async_remote_copy(
            src_ref=pst.at[it], dst_ref=pbuf.at[it, col],
            send_sem=p_send.at[it, e], recv_sem=p_recv.at[it, e],
            device_id=(me, flip(col, e)), device_id_type=MESH)

    for it in range(ITERS):
        part = product(y, 1)
        mass = jnp.broadcast_to(jnp.sum(y, axis=1, keepdims=True), (1, 128))
        gst[it, :, 0:NJ] = part
        gst[it, :, NJ:] = mass
        for e in range(1, S):
            g_copy(it, e).start()
        gbuf[it, me] = gst[it]
        for e in range(1, S):
            g_copy(it, e).wait_recv()
        g = gbuf[it, 0]
        for s in range(1, S):
            g = g + gbuf[it, s]
        x_new = jnp.clip(x - PRIMAL_STEP * (cost[...] - g[:, 0:NJ] / root_scen), -1.0, 1.0)
        z_new = z - THRESH_STEP * (1.0 - g[:, NJ:NJ + 1] / tail)
        x_bar = 2.0 * x_new - x
        z_bar = 2.0 * z_new - z
        pst[it] = product(x_bar, 0)
        for e in range(1, O):
            p_copy(it, e).start()
        pbuf[it, col] = pst[it]
        for e in range(1, O):
            p_copy(it, e).wait_recv()
        p = pbuf[it, 0]
        for o in range(1, O):
            p = p + pbuf[it, o]
        y = jnp.clip(y + DUAL_STEP * (base[...] - p / root_opt - z_bar), 0.0, 1.0)
        x, z = x_new, z_new
    x_out[...] = x
    y_out[...] = y
    z_out[...] = z

    for e in range(1, S):
        for i in range(2):
            prm_a(e, i).wait_send()
    for e in range(1, O):
        prm_b(e).wait_send()
    for kc in range(NK):
        for h in range(2):
            for held, later in plan(h):
                for d in later:
                    piece(kc, h, held, d).wait_send()
    for it in range(ITERS):
        for e in range(1, S):
            g_copy(it, e).wait_send()
        for e in range(1, O):
            p_copy(it, e).wait_send()


def on_device(
    option_coefs,
    underlying_of,
    log_return_mean,
    log_return_spread,
    cost,
    positions,
    base_loss,
    duals,
    threshold,
):
    S = lax.axis_size("scen")
    O = lax.axis_size("opt")
    D = S * O
    B, T = option_coefs.shape
    SC = duals.shape[0]
    NJ = S * B
    limit = max(2, 2 * B // D)
    SL = S * limit
    R = D * SL
    KC = min(CHUNK, T)
    NK = T // KC
    vmem = pl.BlockSpec(memory_space=pltpu.VMEM)
    dma = pltpu.SemaphoreType.DMA
    high, low, x, y, z = pl.pallas_call(
        functools.partial(kernel, (S, O, limit)),
        out_shape=(
            jax.ShapeDtypeStruct((NJ, SC), BF16),
            jax.ShapeDtypeStruct((NJ, SC), BF16),
            jax.ShapeDtypeStruct((1, NJ), F32),
            jax.ShapeDtypeStruct((1, SC), F32),
            jax.ShapeDtypeStruct((1, 1), F32),
        ),
        in_specs=[pl.BlockSpec(memory_space=pl.ANY)] + [vmem] * 8,
        out_specs=(vmem,) * 5,
        scratch_shapes=[
            pltpu.VMEM((NK, S, B, KC), F32),
            pltpu.VMEM((O, S, 2, 1, SC), F32),
            pltpu.VMEM((D, 8 * NK, SC), F32),
            pltpu.VMEM((D, 8 * NK, SC), F32),
            pltpu.VMEM((D, KC // 16, SC), F32),
            pltpu.VMEM((D, KC // 16, SC), F32),
            pltpu.VMEM((T, SC), F32),
            pltpu.VMEM((R, NJ), BF16),
            pltpu.VMEM((NJ, R), BF16),
            pltpu.VMEM((NJ, 2 * KC), BF16),
            pltpu.VMEM((D, 2 * SL, KC), BF16),
            pltpu.VMEM((D, SL, SC), F32),
            pltpu.VMEM((R, 2 * SC), BF16),
            pltpu.VMEM((ITERS, 1, NJ + 128), F32),
            pltpu.VMEM((ITERS, S, 1, NJ + 128), F32),
            pltpu.VMEM((ITERS, 1, SC), F32),
            pltpu.VMEM((ITERS, O, 1, SC), F32),
            dma((NK, 2, S)),
            dma((NK, 2, S)),
            dma((NK,)),
            dma((2,)),
            dma((S, 2)),
            dma((S, 2)),
            dma((O,)),
            dma((O,)),
            dma((ITERS, S)),
            dma((ITERS, S)),
            dma((ITERS, O)),
            dma((ITERS, O)),
        ],
        compiler_params=pltpu.CompilerParams(
            collective_id=0, has_side_effects=True, vmem_limit_bytes=60000 * 1024
        ),
        name="hedge",
    )(
        option_coefs,
        log_return_mean,
        log_return_spread,
        underlying_of.reshape(S, 1, B),
        cost.reshape(1, NJ),
        positions.reshape(1, NJ),
        base_loss.reshape(1, SC),
        duals.reshape(1, SC),
        threshold.reshape(1, 1),
    )
    values = high.astype(F32) + low.astype(F32)
    return (values, x.reshape(NJ), y.reshape(SC), z.reshape(1))


def solution(mesh):
    in_specs = (
        P(("opt", "scen"), None),
        P("opt", None),
        P(("scen", "opt"), None),
        P(("scen", "opt"), None),
        P("opt"),
        P("opt"),
        P("scen"),
        P("scen"),
        P(),
    )
    out_specs = (P("opt", "scen"), P("opt"), P("scen"), P())
    return jax.shard_map(
        on_device, mesh=mesh, in_specs=in_specs, out_specs=out_specs, check_vma=False
    )
```
